32 devices in a mesh: grp: 4 (over y, x), ep: 8 (over z, core).
Axes of the slice: x: 2, y: 2, z: 4, core: 2. Of those that a mesh axis runs over, the one named last changes fastest.
Arguments:
- layer_input: bfloat16 [8192, 8192], P(('grp', 'ep')), may hold values from -6 to 6
- output_grad: bfloat16 [8192, 8192], P(('grp', 'ep')), may hold values from -0.119628906 to 0.119628906
- adapter_ids: int32 [8192, 1], P(('grp', 'ep')), may hold values from 0 to 7; in each aligned block of 256 rows (0 to 255, 256 to 511, ...) at most 64 rows name the same one
- owner_map: int32 [8], replicated, may hold values from 0 to 7, each once
- weights: bfloat16 [8, 2, 64, 8192], P('ep', None, None, 'grp'), may hold values from -0.0625 to 0.0625
- moment: float32 [8, 2, 64, 8192], P('ep', None, None, 'grp'), may hold values from -1.8 to 1.8
- second: float32 [8, 2, 64, 8192], P('ep', None, None, 'grp'), may hold values from 0.0002 to 0.004
Outputs:
- moment_next: float32 [8, 2, 64, 8192], P('ep', None, None, 'grp')
- second_next: float32 [8, 2, 64, 8192], P('ep', None, None, 'grp')
- direction: float32 [8, 2, 64, 8192], P('ep', None, None, 'grp')
The draws below stay inside these ranges and needn't reach their ends.
Inputs may be any that keep to these rules, and one draw needn't show every extreme that they name: `adapter_ids`: among the rows of one device no adapter appears more than 64 times, and some adapter appears exactly 64 times. `owner_map`: each owner index appears once.
All inputs are finite; a program needn't handle non-finite values.
Results may differ from the reference program's by a relative error of at most 0.0026.
Values may be sent and summed in bfloat16 or wider, within the bound.
No kernel may reach another device: no remote copies, remote signals or barrier semaphores. Data moves between devices by JAX's collectives and lax.ppermute only.
A program may use at most 128 MiB of HBM per device.

```python
import math
import jax
import jax.numpy as jnp
import numpy as np
from jax import lax

D = 8192
R = 64
TOK_DEV = 256
STEP = 100
CAP = 64
ADAPTERS = 8
TOKENS = 8192
N_GRP = 4
N_EP = 8


def shard_levels(key, shape, cuts, smallest, largest):
    loudness, own = 1.0, jax.random.fold_in(key, 6)
    for dim, parts in cuts:
        steps = jnp.exp(jax.random.uniform(jax.random.fold_in(own, dim), (parts,), jnp.float32, smallest / len(cuts), largest / len(cuts)))
        loudness = loudness * jnp.repeat(steps, shape[dim] // parts).reshape([-1 if axis == dim else 1 for axis in range(len(shape))])
    return loudness


def assign_block(key, own, number, rows, amount, top, limit, skew):
    sequence = jax.random.permutation(key, amount)
    heavy_load, usual = load_shares(amount, rows * top, limit, skew, True), load_shares(amount, rows * top, limit, skew, False)
    places = jnp.arange(amount)

    def named(tallies, rotation):
        used = int((tallies > 0).sum())
        fixed = max(1, used // 4)
        shifted = fixed + (places - fixed + rotation * (used - fixed)) % max(1, amount - fixed)
        return jnp.zeros((amount,), jnp.int32).at[sequence[jnp.where(places < fixed, places, shifted)]].set(jnp.asarray(tallies, jnp.int32))

    tallies = jnp.where(number % 4 == 0, named(heavy_load, number // 4), named(usual, number - number // 4 - 1))
    mixed = jax.random.permutation(jax.random.fold_in(own, 3), amount)
    source_of, taker = mixed[0:amount // 2 * 2:2], mixed[1:amount // 2 * 2:2]
    room = jnp.minimum(tallies[source_of] - 1, limit - tallies[taker]) // 2
    room = jnp.where((source_of == sequence[0]) | (taker == sequence[0]) | (tallies[taker] == 0), 0, jnp.maximum(room, 0))
    shifted = jax.random.randint(jax.random.fold_in(own, 4), (amount // 2,), 0, 1 << 20) % (room + 1)
    tallies = tallies.at[source_of].add(-shifted).at[taker].add(shifted)
    labels = jnp.searchsorted(jnp.cumsum(tallies), jnp.arange(rows * top), side="right").astype(jnp.int32)
    grid = labels.reshape(top, rows).T
    grid = grid[jax.random.permutation(jax.random.fold_in(own, 1), rows)]
    rotation = jax.random.randint(jax.random.fold_in(own, 2), (rows, 1), 0, top)
    return jnp.take_along_axis(grid, (jnp.arange(top)[None, :] + rotation) % top, axis=1)


def load_shares(count, total, bound, lean, full):
    weights = [(1 << 20) // math.isqrt(rank ** lean) + 1 for rank in range(1, count + 1)]
    largest = bound if full else min(bound, max(-(-total // count), total * weights[0] // sum(weights)))
    least = 1 if total - largest >= count - 1 else 0
    holding, spare = [largest] + [least] * (count - 1), total - largest - least * (count - 1)
    while spare > 0:
        movable = [i for i in range(1, count) if holding[i] < largest] or [i for i in range(1, count) if holding[i] < bound]
        pool, remaining = sum([weights[i] for i in movable]), spare
        for i in movable:
            more = min(bound - holding[i], max(1, remaining * weights[i] // pool), spare)
            holding[i] = holding[i] + more
            spare = spare - more
    return np.array(holding)


def centred(rng, shape, width, reach, cuts=(), held_as=jnp.bfloat16):
    values = width * jax.random.normal(rng, shape, jnp.float32)
    if cuts:
        values = values * shard_levels(rng, shape, cuts, -0.22, 0.18)
    return jnp.clip(values, -reach, reach).astype(held_as)


def setup_inputs(seed: int = 0) -> dict:
    key_list = jax.random.split(jax.random.key(seed), 8)
    layer_input = centred(key_list[0], (TOKENS, D), 1.0, 6.0, ((0, 32),))
    output_grad = centred(key_list[1], (TOKENS, D), 0.02, 0.119628906, ((0, 32),))
    adapter_ids_keys = jax.random.split(jax.random.fold_in(key_list[2], 1), TOKENS // TOK_DEV)
    adapter_ids_turns = jax.random.permutation(jax.random.fold_in(key_list[2], 3), TOKENS // TOK_DEV)
    adapter_ids = jax.vmap(lambda own, number: assign_block(jax.random.fold_in(key_list[2], 2), own, number, TOK_DEV, ADAPTERS, 1, CAP, 2))(adapter_ids_keys, adapter_ids_turns).reshape((TOKENS, 1))
    owner_map = jax.random.permutation(key_list[3], ADAPTERS).astype(jnp.int32)
    weights = centred(key_list[4], (ADAPTERS, 2, R, D), D ** -0.5, 0.0625, ((0, 8), (3, 4)))
    moment = centred(key_list[5], (ADAPTERS, 2, R, D), 0.3, 1.8, ((0, 8), (3, 4)), jnp.float32)
    second = jnp.clip(jnp.exp(math.log(0.004) - 2.9957323 * jax.random.uniform(key_list[6], (ADAPTERS, 2, R, D), jnp.float32) ** shard_levels(key_list[6], (ADAPTERS, 2, R, D), ((0, 8), (3, 4)), -0.2, 0.2)), 0.0002, 0.004)
    return {"layer_input": layer_input, "output_grad": output_grad, "adapter_ids": adapter_ids, "owner_map": owner_map, "weights": weights, "moment": moment, "second": second}


ADAPTER_SCALING = 2.0
BETA_FIRST = 0.9
BETA_SECOND = 0.999
ADAM_EPSILON = 1e-08

def reference(layer_input, output_grad, adapter_ids, owner_map, weights, moment, second):
    total_rows = layer_input.shape[0]
    owner_total = ADAPTERS
    most_rows = N_GRP * N_EP * CAP
    owner_of = owner_map[adapter_ids[:, 0]].astype(jnp.int32)
    owner_hot = (owner_of[:, None] == jnp.arange(owner_total, dtype=jnp.int32)[None, :]).astype(jnp.int32)
    position = lax.optimization_barrier(jnp.sum((jnp.cumsum(owner_hot, axis=0) - 1) * owner_hot, axis=1)).astype(jnp.int32)
    slot_index = (owner_of * most_rows + position).astype(jnp.int32)
    table = jnp.full((owner_total * most_rows,), total_rows, jnp.int32)
    table = table.at[slot_index].set(jnp.arange(total_rows, dtype=jnp.int32)).reshape(owner_total, most_rows)
    padded_input = jnp.concatenate([layer_input, jnp.zeros((1, D), layer_input.dtype)], axis=0)
    padded_grad = jnp.concatenate([output_grad, jnp.zeros((1, D), output_grad.dtype)], axis=0)

    def per_owner(packed):
        index_row, weight_pair = packed
        input_rows = padded_input[index_row]
        incoming_gradients = padded_grad[index_row]
        reduced_input = jnp.dot(input_rows, weight_pair[0].T, preferred_element_type=jnp.float32).astype(jnp.bfloat16)
        reduced_gradient = jnp.dot(incoming_gradients, weight_pair[1].T, preferred_element_type=jnp.float32).astype(jnp.bfloat16)
        down_gradient = ADAPTER_SCALING * jnp.dot(reduced_gradient.T, input_rows, preferred_element_type=jnp.float32)
        up_gradient = ADAPTER_SCALING * jnp.dot(reduced_input.T, incoming_gradients, preferred_element_type=jnp.float32)
        return jnp.stack([down_gradient, up_gradient])
    grads = lax.map(per_owner, (table, weights))
    moment_next = BETA_FIRST * moment + (1.0 - BETA_FIRST) * grads
    second_next = BETA_SECOND * second + (1.0 - BETA_SECOND) * grads * grads
    first_fix = 1.0 - BETA_FIRST ** STEP
    second_fix = 1.0 - BETA_SECOND ** STEP
    direction = moment_next / first_fix / (jnp.sqrt(second_next / second_fix) + ADAM_EPSILON)
    return (moment_next, second_next, direction)
```

```python
import jax
import jax.numpy as jnp
from jax import lax
from jax.sharding import PartitionSpec as P

STEP = 100
ADAPTER_SCALING = 2.0
BETA_FIRST = 0.9
BETA_SECOND = 0.999
ADAM_EPSILON = 1e-08
FEATURE_CHUNKS = 4
RANK_CHUNKS = 4


def swap(values, axis, step):
    count = lax.axis_size(axis)
    return lax.ppermute(values, axis, [(i, i ^ step) for i in range(count)])


def tie(value, *others):
    return lax.optimization_barrier((value, *others))[0]


def adam_step(grads, moment, second):
    moment_next = BETA_FIRST * moment + (1.0 - BETA_FIRST) * grads
    second_next = BETA_SECOND * second + (1.0 - BETA_SECOND) * grads * grads
    first_fix = 1.0 - BETA_FIRST**STEP
    second_fix = 1.0 - BETA_SECOND**STEP
    direction = moment_next / first_fix / (jnp.sqrt(second_next / second_fix) + ADAM_EPSILON)
    return (moment_next, second_next, direction)


def gather_owners(own):
    count = lax.axis_size("ep")
    even = [own] + [swap(own, "ep", k) for k in range(2, count, 2)]
    even = jnp.stack(even)
    odd = swap(even, "ep", 1)
    return jnp.stack([even, odd], axis=1).reshape((count,) + own.shape)


def scatter_owners(partial):
    count = lax.axis_size("ep")
    pairs = partial.reshape((count // 2, 2) + partial.shape[1:])
    here = pairs[:, 0] + swap(pairs[:, 1].astype(jnp.bfloat16), "ep", 1).astype(jnp.float32)
    total = here[0]
    sent = here.astype(jnp.bfloat16)
    for k in range(1, count // 2):
        total = total + swap(sent[k], "ep", 2 * k).astype(jnp.float32)
    return total


def per_device(layer_input, output_grad, adapter_ids, owner_map, weights, moment, second):
    groups = lax.axis_size("grp")
    owners = lax.axis_size("ep")
    mine = lax.axis_index("grp")
    me = lax.axis_index("ep")
    rows, width = layer_input.shape
    part = width // groups
    rank = weights.shape[2]

    def piece(array, step, chunk, chunks):
        size = part // chunks
        return lax.dynamic_slice(array, (0, (mine ^ step) * part + chunk * size), (rows, size))

    hot = adapter_ids[:, 0][None, :] == jnp.arange(owner_map.shape[0], dtype=jnp.int32)[:, None]
    owner_of = jnp.sum(jnp.where(hot, owner_map[:, None], 0), axis=0)
    owner_of = jnp.concatenate([owner_of] + [swap(owner_of, "grp", d) for d in range(1, groups)])
    relative = owner_of ^ me
    mask = relative[None, :] == jnp.arange(owners, dtype=jnp.int32)[:, None]

    def send(array, chunk, chunks, after=None):
        out = [piece(array, 0, chunk, chunks)]
        for d in range(1, groups):
            block = piece(array, d, chunk, chunks)
            if after is not None:
                block = tie(block, after)
            out.append(swap(block, "grp", d))
        return jnp.concatenate(out)

    def low_part(matrix, values):
        every = lax.dot_general(
            matrix.reshape(owners * rank, -1), values, (((1,), (1,)), ((), ())), preferred_element_type=jnp.float32
        ).reshape(owners, rank, -1)
        return jnp.sum(jnp.where(mask[:, None, :], every, 0.0), axis=0)

    def blocks(low):
        return [low[:, b * rows : (b + 1) * rows] for b in range(groups)]

    def sum_two_stage(low):
        part_of = blocks(low)
        total = part_of[0]
        for d in range(1, groups):
            total = total + swap(part_of[d], "grp", d)
        total = total.astype(jnp.bfloat16)
        return jnp.concatenate([total] + [swap(total, "grp", d) for d in range(1, groups)], axis=1)

    def sum_direct(low):
        got = [blocks(low)] + [blocks(swap(low, "grp", d)) for d in range(1, groups)]
        out = []
        for b in range(groups):
            total = got[0][b]
            for d in range(1, groups):
                total = total + got[d][b ^ d]
            out.append(total)
        return jnp.concatenate(out, axis=1).astype(jnp.bfloat16)

    def outer(low, values):
        spread = jnp.where(mask[:, None, :], low[None], jnp.zeros((), low.dtype))
        return ADAPTER_SCALING * lax.dot_general(
            spread.reshape(-1, low.shape[1]), values, (((1,), (0,)), ((), ())), preferred_element_type=jnp.float32
        ).reshape(owners, low.shape[0], -1)

    cut = part // FEATURE_CHUNKS
    og = send(output_grad, 0, 1)
    up = gather_owners(weights[0, 1])
    down = gather_owners(weights[0, 0])
    li = [send(layer_input, 0, FEATURE_CHUNKS)]
    grad_part = low_part(up, og)
    low_grad = sum_two_stage(grad_part)
    gate = grad_part
    for c in range(1, FEATURE_CHUNKS):
        li.append(send(layer_input, c, FEATURE_CHUNKS, after=gate))
        gate = li[c - 1] if c > 1 else li[0]
    down_grads = []
    low_in = None
    for c in range(FEATURE_CHUNKS):
        p = low_part(down[:, :, c * cut : (c + 1) * cut], li[c])
        low_in = p if low_in is None else low_in + p
        down_grads.append(scatter_owners(outer(low_grad, li[c])))
    down_grad = jnp.concatenate(down_grads, axis=1)
    size = rank // RANK_CHUNKS
    up_grads = []
    for r in range(RANK_CHUNKS):
        low = sum_direct(low_in[r * size : (r + 1) * size])
        up_grads.append(scatter_owners(outer(low, og)))
    up_grad = jnp.concatenate(up_grads, axis=0)
    grads = jnp.stack([down_grad, up_grad])[None]
    return adam_step(grads, moment, second)


def solution(mesh):
    rows = P(("grp", "ep"), None)
    held = P("ep", None, None, "grp")
    return jax.shard_map(
        per_device,
        mesh=mesh,
        in_specs=(rows, rows, rows, P(), held, held, held),
        out_specs=(held, held, held),
        check_vma=False,
    )
```

```python
import jax
import jax.numpy as jnp
from jax import lax
from jax.sharding import PartitionSpec as P

STEP = 100
ADAPTER_SCALING = 2.0
BETA_FIRST = 0.9
BETA_SECOND = 0.999
ADAM_EPSILON = 1e-08
FEATURE_CHUNKS = 4
RANK_CHUNKS = 2


def swap(values, axis, step):
    count = lax.axis_size(axis)
    return lax.ppermute(values, axis, [(i, i ^ step) for i in range(count)])


def tie(value, *others):
    return lax.optimization_barrier((value, *others))[0]


def adam_step(grads, moment, second):
    moment_next = BETA_FIRST * moment + (1.0 - BETA_FIRST) * grads
    second_next = BETA_SECOND * second + (1.0 - BETA_SECOND) * grads * grads
    first_fix = 1.0 - BETA_FIRST**STEP
    second_fix = 1.0 - BETA_SECOND**STEP
    direction = moment_next / first_fix / (jnp.sqrt(second_next / second_fix) + ADAM_EPSILON)
    return (moment_next, second_next, direction)


def gather_owners(own):
    count = lax.axis_size("ep")
    even = [own] + [swap(own, "ep", k) for k in range(2, count, 2)]
    even = jnp.stack(even)
    odd = swap(even, "ep", 1)
    return jnp.stack([even, odd], axis=1).reshape((count,) + own.shape)


def scatter_owners(partial):
    count = lax.axis_size("ep")
    pairs = partial.reshape((count // 2, 2) + partial.shape[1:])
    here = pairs[:, 0] + swap(pairs[:, 1].astype(jnp.bfloat16), "ep", 1).astype(jnp.float32)
    total = here[0]
    sent = here.astype(jnp.bfloat16)
    for k in range(1, count // 2):
        total = total + swap(sent[k], "ep", 2 * k).astype(jnp.float32)
    return total


def per_device(layer_input, output_grad, adapter_ids, owner_map, weights, moment, second):
    groups = lax.axis_size("grp")
    owners = lax.axis_size("ep")
    mine = lax.axis_index("grp")
    me = lax.axis_index("ep")
    rows, width = layer_input.shape
    part = width // groups
    rank = weights.shape[2]

    def piece(array, step, chunk, chunks):
        size = part // chunks
        return lax.dynamic_slice(array, (0, (mine ^ step) * part + chunk * size), (rows, size))

    def send(array, chunk, chunks, after=None):
        out = [piece(array, 0, chunk, chunks)]
        for d in range(1, groups):
            block = piece(array, d, chunk, chunks)
            if after is not None:
                block = tie(block, after)
            out.append(swap(block, "grp", d))
        return jnp.concatenate(out)

    og = send(output_grad, 0, 1)
    li = [send(layer_input, 0, FEATURE_CHUNKS)]

    hot = adapter_ids[:, 0][None, :] == jnp.arange(owner_map.shape[0], dtype=jnp.int32)[:, None]
    owner_of = jnp.sum(jnp.where(hot, owner_map[:, None], 0), axis=0)
    owner_of = jnp.concatenate([owner_of] + [swap(owner_of, "grp", d) for d in range(1, groups)])
    relative = owner_of ^ me
    mask = relative[None, :] == jnp.arange(owners, dtype=jnp.int32)[:, None]

    def low_part(matrix, values):
        every = lax.dot_general(
            matrix.reshape(owners * rank, -1), values, (((1,), (1,)), ((), ())), preferred_element_type=jnp.float32
        ).reshape(owners, rank, -1)
        return jnp.sum(jnp.where(mask[:, None, :], every, 0.0), axis=0)

    def blocks(low):
        return [low[:, b * rows : (b + 1) * rows] for b in range(groups)]

    def sum_two_stage(low):
        part_of = blocks(low)
        total = part_of[0]
        for d in range(1, groups):
            total = total + swap(part_of[d], "grp", d)
        total = total.astype(jnp.bfloat16)
        return jnp.concatenate([total] + [swap(total, "grp", d) for d in range(1, groups)], axis=1)

    def sum_direct(low):
        got = [blocks(low)] + [blocks(swap(low, "grp", d)) for d in range(1, groups)]
        out = []
        for b in range(groups):
            total = got[0][b]
            for d in range(1, groups):
                total = total + got[d][b ^ d]
            out.append(total)
        return jnp.concatenate(out, axis=1).astype(jnp.bfloat16)

    def outer(low, values):
        spread = jnp.where(mask[:, None, :], low[None], jnp.zeros((), low.dtype))
        return ADAPTER_SCALING * lax.dot_general(
            spread.reshape(-1, low.shape[1]), values, (((1,), (0,)), ((), ())), preferred_element_type=jnp.float32
        ).reshape(owners, low.shape[0], -1)

    cut = part // FEATURE_CHUNKS
    up = gather_owners(weights[0, 1])
    down = gather_owners(weights[0, 0])
    low_grad = sum_two_stage(low_part(up, og))
    for c in range(1, FEATURE_CHUNKS):
        li.append(send(layer_input, c, FEATURE_CHUNKS))
    low_in = None
    for c in range(FEATURE_CHUNKS):
        p = low_part(down[:, :, c * cut : (c + 1) * cut], li[c])
        low_in = p if low_in is None else low_in + p
    down_grads = []
    half = FEATURE_CHUNKS // 2
    pair = jnp.concatenate([outer(low_grad, li[c]) for c in range(half)], axis=2)
    down_grads.append(scatter_owners(pair))
    for c in range(half, FEATURE_CHUNKS):
        down_grads.append(scatter_owners(outer(low_grad, li[c])))
    down_grad = jnp.concatenate(down_grads, axis=1)
    size = rank // RANK_CHUNKS
    up_grads = []
    for r in range(RANK_CHUNKS):
        low = sum_direct(low_in[r * size : (r + 1) * size])
        up_grads.append(scatter_owners(outer(low, og)))
    up_grad = jnp.concatenate(up_grads, axis=0)
    grads = jnp.stack([down_grad, up_grad])[None]
    return adam_step(grads, moment, second)


def solution(mesh):
    rows = P(("grp", "ep"), None)
    held = P("ep", None, None, "grp")

    return jax.shard_map(
        per_device,
        mesh=mesh,
        in_specs=(rows, rows, rows, P(), held, held, held),
        out_specs=(held, held, held),
        check_vma=False,
    )
```

```python
import jax
import jax.numpy as jnp
from jax import lax
from jax.sharding import PartitionSpec as P

STEP = 100
ADAPTER_SCALING = 2.0
BETA_FIRST = 0.9
BETA_SECOND = 0.999
ADAM_EPSILON = 1e-08
FEATURE_CHUNKS = 4
RANK_CHUNKS = 2


def swap(values, axis, step):
    count = lax.axis_size(axis)
    return lax.ppermute(values, axis, [(i, i ^ step) for i in range(count)])


def adam_step(grads, moment, second):
    moment_next = BETA_FIRST * moment + (1.0 - BETA_FIRST) * grads
    second_next = BETA_SECOND * second + (1.0 - BETA_SECOND) * grads * grads
    first_fix = 1.0 - BETA_FIRST**STEP
    second_fix = 1.0 - BETA_SECOND**STEP
    direction = moment_next / first_fix / (jnp.sqrt(second_next / second_fix) + ADAM_EPSILON)
    return (moment_next, second_next, direction)


def gather_owners(own):
    count = lax.axis_size("ep")
    even = [own] + [swap(own, "ep", k) for k in range(2, count, 2)]
    even = jnp.stack(even)
    odd = swap(even, "ep", 1)
    return jnp.stack([even, odd], axis=1).reshape((count,) + own.shape)


def scatter_owners(partial):
    count = lax.axis_size("ep")
    pairs = partial.reshape((count // 2, 2) + partial.shape[1:])
    here = pairs[:, 0] + swap(pairs[:, 1].astype(jnp.bfloat16), "ep", 1).astype(jnp.float32)
    total = here[0]
    sent = here.astype(jnp.bfloat16)
    for k in range(1, count // 2):
        total = total + swap(sent[k], "ep", 2 * k).astype(jnp.float32)
    return total


def per_device(layer_input, output_grad, adapter_ids, owner_map, weights, moment, second):
    groups = lax.axis_size("grp")
    owners = lax.axis_size("ep")
    mine = lax.axis_index("grp")
    me = lax.axis_index("ep")
    rows, width = layer_input.shape
    part = width // groups
    rank = weights.shape[2]

    def piece(array, step, chunk, chunks):
        size = part // chunks
        return lax.dynamic_slice(array, (0, (mine ^ step) * part + chunk * size), (rows, size))

    def send(array, chunk, chunks, single=False):
        out = []
        for d in range(1, groups):
            block = piece(array, d, chunk, chunks)
            if single:
                array, block = lax.optimization_barrier((array, block))
            out.append(swap(block, "grp", d))
        return jnp.concatenate([piece(array, 0, chunk, chunks)] + out)

    og = send(output_grad, 0, 1)
    li = [send(layer_input, 0, FEATURE_CHUNKS)]

    hot = adapter_ids[:, 0][None, :] == jnp.arange(owner_map.shape[0], dtype=jnp.int32)[:, None]
    owner_of = jnp.sum(jnp.where(hot, owner_map[:, None], 0), axis=0)
    owner_of = jnp.concatenate([owner_of] + [swap(owner_of, "grp", d) for d in range(1, groups)])
    relative = owner_of ^ me
    mask = relative[None, :] == jnp.arange(owners, dtype=jnp.int32)[:, None]

    def low_part(matrix, values):
        every = lax.dot_general(
            matrix.reshape(owners * rank, -1), values, (((1,), (1,)), ((), ())), preferred_element_type=jnp.float32
        ).reshape(owners, rank, -1)
        return jnp.sum(jnp.where(mask[:, None, :], every, 0.0), axis=0)

    def blocks(low):
        return [low[:, b * rows : (b + 1) * rows] for b in range(groups)]

    def sum_two_stage(low):
        part_of = blocks(low)
        total = part_of[0]
        for d in range(1, groups):
            total = total + swap(part_of[d], "grp", d)
        total = total.astype(jnp.bfloat16)
        return jnp.concatenate([total] + [swap(total, "grp", d) for d in range(1, groups)], axis=1)

    def sum_direct(low):
        got = [blocks(low)] + [blocks(swap(low, "grp", d)) for d in range(1, groups)]
        out = []
        for b in range(groups):
            total = got[0][b]
            for d in range(1, groups):
                total = total + got[d][b ^ d]
            out.append(total)
        return jnp.concatenate(out, axis=1).astype(jnp.bfloat16)

    def outer(low, values):
        spread = jnp.where(mask[:, None, :], low[None], jnp.zeros((), low.dtype))
        return ADAPTER_SCALING * lax.dot_general(
            spread.reshape(-1, low.shape[1]), values, (((1,), (0,)), ((), ())), preferred_element_type=jnp.float32
        ).reshape(owners, low.shape[0], -1)

    cut = part // FEATURE_CHUNKS
    up = gather_owners(weights[0, 1])
    down = gather_owners(weights[0, 0])
    low_grad = sum_two_stage(low_part(up, og))
    for c in range(1, FEATURE_CHUNKS):
        li.append(send(layer_input, c, FEATURE_CHUNKS))
    low_in = None
    for c in range(FEATURE_CHUNKS):
        p = low_part(down[:, :, c * cut : (c + 1) * cut], li[c])
        low_in = p if low_in is None else low_in + p
    down_grads = []
    half = FEATURE_CHUNKS // 2
    pair = jnp.concatenate([outer(low_grad, li[c]) for c in range(half)], axis=2)
    down_grads.append(scatter_owners(pair))
    for c in range(half, FEATURE_CHUNKS):
        down_grads.append(scatter_owners(outer(low_grad, li[c])))
    down_grad = jnp.concatenate(down_grads, axis=1)
    size = rank // RANK_CHUNKS
    og_all = lax.optimization_barrier(og)
    up_grads = []
    for r in range(RANK_CHUNKS):
        low = sum_direct(low_in[r * size : (r + 1) * size])
        up_grads.append(scatter_owners(outer(low, og_all)))
    up_grad = jnp.concatenate(up_grads, axis=0)
    grads = jnp.stack([down_grad, up_grad])[None]
    return adam_step(grads, moment, second)


def solution(mesh):
    rows = P(("grp", "ep"), None)
    held = P("ep", None, None, "grp")

    return jax.shard_map(
        per_device,
        mesh=mesh,
        in_specs=(rows, rows, rows, P(), held, held, held),
        out_specs=(held, held, held),
        check_vma=False,
    )
```
